32 devices in a mesh: heads: 2 (over core), tm: 16 (over z, y, x).
Axes of the slice: x: 2, y: 2, z: 4, core: 2. Of those that a mesh axis runs over, the one named last changes fastest.
Arguments:
- queries: bfloat16 [4096, 768], P('tm', 'heads'), parts along dimension 1, may hold values from -8 to 8
- keys: bfloat16 [4096, 768], P('tm', 'heads'), parts along dimension 1, may hold values from -8 to 8
- values: bfloat16 [4096, 768], P('tm', 'heads'), parts along dimension 1, may hold values from -6 to 6
- positions: int32 [3, 4096], P(None, 'tm'), may hold values from 0 to 79, as said below
- tile_masks: int32 [32, 8, 2], P('tm'), may hold values from 0 to 1, as said below
- sink_index: int32 [256], replicated, may hold values from 0 to 3599, as said below
Outputs:
- attended: bfloat16 [4096, 768], P('tm', 'heads'), parts along dimension 1
The draws below stay inside these ranges and needn't reach their ends.
There are 2 independent parts, one for each index of `heads`. The reference program is written for one: setup_inputs(seed, part) draws one part's arguments, and reference() takes and returns one part's arrays. A program takes and returns all parts, laid end to end along the dimension named above; an argument that names none is the same for every part. Nothing has to cross between parts.
Inputs may be any that keep to these rules, and one draw needn't show every extreme that they name: `positions`: consecutive tokens of the latent video of 33 x 45 x 80, row by row, from some starting token. `tile_masks`: tiles of farther partners are kept less often. `sink_index`: distinct rows among the first min(4096, 3600) of the window.
All inputs are finite; a program needn't handle non-finite values.
Results may differ from the reference program's by a relative error of at most 0.0085.
The reference program's roundings to bfloat16 on the way count: a program that leaves them out, or rounds other values in their place, can miss the bound.
Values may be sent and summed in bfloat16 or wider, within the bound.
No kernel may reach another device: no remote copies, remote signals or barrier semaphores. Data moves between devices by JAX's collectives and lax.ppermute only.
A program may use at most 64 MiB of HBM per device.

```python
import jax
import jax.numpy as jnp
from jax import lax

HG = 3
HD = 128
TILE = 128
NOFF = 4
SINK = 256
LAT_T = 33
LAT_H = 45
LAT_W = 80
TOK_DEV = 256
TOKENS = 4096
N_TM = 16


def paired_draw(key):
    base = jax.random.fold_in(key, 7)
    first_key, second_key = jax.random.split(base, 2)
    feature_width = HG * HD
    query_data = jnp.clip(jax.random.normal(first_key, (TOKENS, feature_width)), -6.0, 6.0)
    key_data = jnp.clip(jax.random.normal(second_key, (TOKENS, feature_width)), -6.0, 6.0)
    return (query_data.astype(jnp.float32), key_data.astype(jnp.float32))


def draw_queries(key, part):
    return paired_draw(key)[0].astype(jnp.bfloat16)


def draw_keys(key, part):
    return paired_draw(key)[1].astype(jnp.bfloat16)


def draw_positions(key, part):
    frame_size = LAT_H * LAT_W
    start_token = jax.random.randint(jax.random.fold_in(key, 3), (), 0, LAT_T * frame_size - TOKENS + 1)
    global_ids = start_token + jnp.arange(TOKENS, dtype=jnp.int32)
    frame_ids = global_ids // frame_size
    row_ids = global_ids // LAT_W % LAT_H
    column_ids = global_ids % LAT_W
    return jnp.stack([frame_ids, row_ids, column_ids], axis=0).astype(jnp.int32)


def draw_tile_masks(key, part):
    tile_draw = jax.random.randint(jax.random.fold_in(key, 5), (TOKENS // TILE, 2 * NOFF, TOK_DEV // TILE), 0, NOFF + 1)
    distance = (jnp.arange(2 * NOFF, dtype=jnp.int32) % NOFF + 1)[None, :, None]
    return (tile_draw < NOFF + 1 - distance).astype(jnp.int32)


def draw_sink_index(key, part):
    first_rows = min(TOKENS, LAT_H * LAT_W)
    shuffled = jax.random.permutation(jax.random.fold_in(key, 9), first_rows - 2) + 1
    middle = shuffled[:SINK - 2].astype(jnp.int32)
    return jnp.concatenate([jnp.zeros((1,), jnp.int32), middle, jnp.full((1,), first_rows - 1, jnp.int32)]).astype(jnp.int32)


def block_levels(stream_key, shape, cuts, least, largest):
    level, own = 1.0, jax.random.fold_in(stream_key, 6)
    for dim, shards_of in cuts:
        draws = jnp.exp(jax.random.uniform(jax.random.fold_in(own, dim), (shards_of,), jnp.float32, least / len(cuts), largest / len(cuts)))
        level = level * jnp.repeat(draws, shape[dim] // shards_of).reshape([-1 if axis == dim else 1 for axis in range(len(shape))])
    return level


def noise(stream_key, dims, spread, limit, cuts=(), held_as=jnp.bfloat16):
    drawn = jax.random.normal(stream_key, dims, jnp.float32) * spread
    if len(cuts) > 0:
        drawn = block_levels(stream_key, dims, cuts, -0.22, 0.18) * drawn
    return jnp.clip(drawn, min=-limit, max=limit).astype(held_as)


def setup_inputs(seed: int = 0, part: int = 0) -> dict:
    key_of = jax.random.split(jax.random.key(seed), 7)
    part_keys = jax.random.split(jax.random.fold_in(key_of[6], part), 7)
    queries = draw_queries(jax.random.fold_in(jax.random.fold_in(key_of[6], part), 71), part)
    keys = draw_keys(jax.random.fold_in(jax.random.fold_in(key_of[6], part), 71), part)
    values = noise(part_keys[2], (TOKENS, HG * HD), 1.0, 6.0, ((0, 16),))
    positions = draw_positions(jax.random.fold_in(key_of[6], 71), part)
    tile_masks = draw_tile_masks(jax.random.fold_in(key_of[6], 71), part)
    sink_index = draw_sink_index(jax.random.fold_in(key_of[6], 71), part)
    return {"queries": queries, "keys": keys, "values": values, "positions": positions, "tile_masks": tile_masks, "sink_index": sink_index}


def rotate(row_data, position, factor):
    row_count = row_data.shape[0]
    first_size = HD // 8
    second_size = (HD - HD // 8) // 2
    section_sizes = (first_size, second_size, HD - first_size - second_size)
    angle_list = []
    for axis_id in range(3):
        section_width = section_sizes[axis_id]
        inverse = 256.0 ** (-jnp.arange(0, section_width, 2).astype(jnp.float32) / section_width)
        angle_list.append(position[axis_id].astype(jnp.float32)[:, None] * inverse[None, :])
    angle_all = jnp.concatenate(angle_list, axis=1)
    cosine = jnp.cos(angle_all)[:, None, :]
    sine_part = jnp.sin(angle_all)[:, None, :]
    pair_view = row_data.astype(jnp.float32).reshape(row_count, HG, HD // 2, 2)
    even_part = pair_view[..., 0]
    odd_part = pair_view[..., 1]
    turned = jnp.stack([even_part * cosine - odd_part * sine_part, even_part * sine_part + odd_part * cosine], axis=-1)
    return (turned * factor).reshape(row_count, HG * HD)


def reference(queries, keys, values, positions, tile_masks, sink_index):
    q_rot = rotate(queries, positions, HD ** -0.5).astype(jnp.bfloat16)
    k_rot = rotate(keys, positions, 1.0).astype(jnp.bfloat16)
    sink_keys = k_rot[sink_index].reshape(SINK, HG, HD)
    sink_values = values[sink_index].reshape(SINK, HG, HD)
    shards = N_TM
    tiles = TOK_DEV // TILE
    query_blocks = q_rot.reshape(shards, TOK_DEV, HG, HD)
    key_blocks = k_rot.reshape(shards, TOK_DEV, HG, HD)
    value_blocks = values.reshape(shards, TOK_DEV, HG, HD)
    mask_blocks = tile_masks.reshape(shards, tiles, 2 * NOFF, tiles)
    offset_list = [0] + list(range(1, NOFF + 1)) + [-step for step in range(1, NOFF + 1)]

    def one_shard(shard_id):
        key_list = []
        value_list = []
        mask_list = []
        for offset in offset_list:
            other = shard_id + offset
            inside = ((other >= 0) & (other < shards)).astype(jnp.float32)
            clipped = jnp.clip(other, 0, shards - 1).astype(jnp.int32)
            key_list.append(key_blocks[clipped])
            value_list.append(value_blocks[clipped])
            if offset == 0:
                tile_keep = jnp.ones((tiles, tiles), jnp.float32)
            elif offset > 0:
                tile_keep = mask_blocks[shard_id][:, offset - 1, :].astype(jnp.float32)
            else:
                tile_keep = mask_blocks[shard_id][:, NOFF - offset - 1, :].astype(jnp.float32)
            mask_list.append(tile_keep * inside)
        key_all = jnp.concatenate(key_list + [sink_keys], axis=0).astype(jnp.float32)
        value_all = jnp.concatenate(value_list + [sink_values], axis=0).astype(jnp.float32)
        keep_tiles = jnp.concatenate(mask_list, axis=1)
        keep_rows = jnp.repeat(jnp.repeat(keep_tiles, TILE, axis=0), TILE, axis=1)
        keep_mask = jnp.concatenate([keep_rows, jnp.ones((TOK_DEV, SINK), jnp.float32)], axis=1)[:, None, :]
        query_here = query_blocks[shard_id].astype(jnp.float32)
        scores = jnp.einsum('qhd,khd->qhk', query_here, key_all, precision=lax.Precision.HIGHEST)
        masked = jnp.where(keep_mask > 0, scores, -1e30)
        row_max = jnp.max(masked, axis=2)
        weights = jnp.exp(masked - row_max[:, :, None]) * keep_mask
        totals = jnp.sum(weights, axis=2)
        rounded = weights.astype(jnp.bfloat16)
        rounded = lax.optimization_barrier(rounded).astype(jnp.float32)
        weighted = jnp.einsum('qhk,khd->qhd', rounded, value_all, precision=lax.Precision.HIGHEST)
        return (weighted / totals[:, :, None]).astype(jnp.bfloat16)

    result = lax.map(one_shard, jnp.arange(shards, dtype=jnp.int32))
    return result.reshape(TOKENS, HG * HD)
```

```python
import functools

import jax
import jax.numpy as jnp
import numpy as np
from jax import lax
from jax.experimental import pallas as pl
from jax.experimental.pallas import tpu as pltpu
from jax.sharding import PartitionSpec as P

HG = 3
HD = 128
TILE = 128
NOFF = 4
PLANE = 4
FW = HG * HD
NEG = -1e30


def rotary_constants():
    first = HD // 8
    second = (HD - first) // 2
    table = np.zeros((8, HD), np.float32)
    at = 0
    for axis_id, width in enumerate((first, second, HD - first - second)):
        inverse = np.power(np.float32(256.0), -np.arange(0, width, 2).astype(np.float32) / np.float32(width))
        table[axis_id, at : at + width] = 1.0
        table[3, at : at + width] = np.repeat(inverse.astype(np.float32), 2)
        at += width
    table[4, 0::2] = -1.0
    table[4, 1::2] = 1.0
    return table


def sin_cos(angle):
    turns = jnp.floor(angle * np.float32(2.0 / np.pi) + np.float32(0.5))
    r = angle - turns * np.float32(1.5703125)
    r = r - turns * np.float32(4.837512969970703125e-4)
    r = r - turns * np.float32(7.54978995489188216e-8)
    z = r * r
    s = r + r * z * (np.float32(-1.6666654611e-1) + z * (np.float32(8.3321608736e-3) + z * np.float32(-1.9515295891e-4)))
    c = 1.0 - 0.5 * z + z * z * (
        np.float32(4.166664568298827e-2) + z * (np.float32(-1.388731625493765e-3) + z * np.float32(2.443315711809948e-5))
    )
    quadrant = turns.astype(jnp.int32)
    swap = (quadrant & 1) == 1
    sin_part = jnp.where(swap, c, s)
    cos_part = jnp.where(swap, s, c)
    sin_part = jnp.where((quadrant & 2) == 2, -sin_part, sin_part)
    cos_part = jnp.where(((quadrant + 1) & 2) == 2, -cos_part, cos_part)
    return sin_part, cos_part


def prep_kernel(base_ref, q_ref, k_ref, v_ref, pos_ref, sink_ref, const_ref, qr_ref, kv_ref, *sink_out):
    rows = q_ref.shape[0]
    const = const_ref[...]
    spread = lax.dot_general(
        pos_ref[...].astype(jnp.float32),
        const[0:3],
        (((0,), (0,)), ((), ())),
        precision=lax.Precision.HIGHEST,
        preferred_element_type=jnp.float32,
    )
    sine, cosine = sin_cos(spread * const[3:4])
    sine = sine * const[4:5]
    even = lax.broadcasted_iota(jnp.int32, (rows, HD), 1) % 2 == 0

    def turned(x):
        x = x.astype(jnp.float32)
        other = jnp.where(even, pltpu.roll(x, HD - 1, 1), pltpu.roll(x, 1, 1))
        return x * cosine + other * sine

    for h in range(HG):
        cols = slice(h * HD, (h + 1) * HD)
        qr_ref[:, cols] = (turned(q_ref[:, cols]) * np.float32(HD ** -0.5)).astype(jnp.bfloat16)
        kv_ref[:, cols] = turned(k_ref[:, cols]).astype(jnp.bfloat16)
    kv_ref[:, FW:] = v_ref[...]
    sinks = sink_ref.shape[1]
    hot = lax.broadcasted_iota(jnp.int32, (rows, sinks), 0) == sink_ref[...] - base_ref[0]
    table = lax.dot_general(
        hot.astype(jnp.float32).astype(jnp.bfloat16),
        kv_ref[...],
        (((0,), (0,)), ((), ())),
        preferred_element_type=jnp.float32,
    ).astype(jnp.bfloat16)
    at = 0
    for out in sink_out:
        out[...] = table[at : at + out.shape[0]]
        at += out.shape[0]


def prepare(base, queries, keys, values, positions, sinks):
    rows = queries.shape[0]
    count = sinks.shape[0]
    vmem = pl.BlockSpec(memory_space=pltpu.VMEM)
    shape = lambda *dims: jax.ShapeDtypeStruct(dims, jnp.bfloat16)
    return pl.pallas_call(
        prep_kernel,
        out_shape=(
            shape(rows, FW),
            shape(rows, 2 * FW),
            shape(count // 2, 2 * FW),
            shape(count // 4, 2 * FW),
            shape(count // 4, 2 * FW),
        ),
        in_specs=[pl.BlockSpec(memory_space=pltpu.SMEM)] + [vmem] * 6,
        out_specs=(vmem,) * 5,
        cost_estimate=pl.CostEstimate(flops=400_000_000, bytes_accessed=1_600_000, transcendentals=0),
        name="prepare",
    )(base, queries, keys, values, positions, sinks.reshape(1, -1), jnp.asarray(rotary_constants()))


def offset_of(name, x, y):
    by_x, by_y = 1 - 2 * x, 1 - 2 * y
    return {
        "X": by_x,
        "Y": 2 * by_y,
        "D": by_x + 2 * by_y,
        "F": 4 * by_y,
        "G": -4 * by_y,
        "V": -2 * by_y,
        "W": -3 * by_x,
        "R": by_x - 2 * by_y,
    }[name]


def attend_kernel(names, first, last, n_blocks, *refs):
    refs = list(refs)
    where_ref = refs.pop(0)
    mask_ref = refs.pop(0)
    q_ref = refs.pop(0)
    blocks = [refs.pop(0) for _ in range(n_blocks)]
    if not first:
        acc_in, m_in, l_in = refs.pop(0), refs.pop(0), refs.pop(0)
    if last:
        out_ref = refs.pop(0)
    else:
        acc_out, m_out, l_out = refs.pop(0), refs.pop(0), refs.pop(0)
    me, shards = where_ref[0], where_ref[1]
    x, y = me & 1, (me >> 1) & 1
    rows = q_ref.shape[0]
    tiles = rows // TILE
    keep = {}
    for b, name in enumerate(names):
        if name in ("own", "sink"):
            continue
        d = offset_of(name, x, y)
        other = me + d
        inside = jnp.logical_and(other >= 0, other < shards)
        slot = jnp.where(d > 0, d - 1, NOFF - 1 - d)
        for qt in range(tiles):
            for kt in range(tiles):
                on = jnp.logical_and(inside, mask_ref[qt, slot, kt] > 0)
                keep[b, qt, kt] = jnp.where(on, 0.0, NEG).astype(jnp.float32)
    for h in range(HG):
        kc = slice(h * HD, (h + 1) * HD)
        vc = slice(FW + h * HD, FW + (h + 1) * HD)
        for qt in range(tiles):
            rs = slice(qt * TILE, (qt + 1) * TILE)
            q = q_ref[rs, kc]
            scores = []
            top = None
            for b, name in enumerate(names):
                s = lax.dot_general(
                    q, blocks[b][:, kc], (((1,), (1,)), ((), ())), preferred_element_type=jnp.float32
                )
                if (b, 0, 0) in keep:
                    s = jnp.concatenate(
                        [s[:, kt * TILE : (kt + 1) * TILE] + keep[b, qt, kt] for kt in range(tiles)], axis=1
                    )
                scores.append(s)
                t = jnp.max(s, axis=1, keepdims=True)
                top = t if top is None else jnp.maximum(top, t)
            if not first:
                old = m_in[rs, h : h + 1]
                top = jnp.maximum(top, old)
                scale = jnp.exp(old - top)
                acc = acc_in[rs, kc] * scale
                total = l_in[rs, h : h + 1] * scale
            else:
                acc = total = None
            for b in range(n_blocks):
                p = jnp.exp(scores[b] - top)
                t = jnp.sum(p, axis=1, keepdims=True)
                total = t if total is None else total + t
                o = jnp.dot(p.astype(jnp.bfloat16), blocks[b][:, vc], preferred_element_type=jnp.float32)
                acc = o if acc is None else acc + o
            if last:
                out_ref[rs, kc] = (acc / total).astype(jnp.bfloat16)
            else:
                acc_out[rs, kc] = acc
                m_out[rs, h : h + 1] = top
                l_out[rs, h : h + 1] = total


def attend(where, masks, q_rot, named, state, last):
    rows = q_rot.shape[0]
    names = tuple(name for name, _ in named)
    arrays = [a for _, a in named]
    first = state is None
    smem = pl.BlockSpec(memory_space=pltpu.SMEM)
    vmem = pl.BlockSpec(memory_space=pltpu.VMEM)
    f32 = lambda *dims: jax.ShapeDtypeStruct(dims, jnp.float32)
    if last:
        out_shape = jax.ShapeDtypeStruct((rows, FW), jnp.bfloat16)
        out_specs = vmem
    else:
        out_shape = (f32(rows, FW), f32(rows, HD), f32(rows, HD))
        out_specs = (vmem,) * 3
    ins = [q_rot] + arrays + ([] if first else list(state))
    n = len(arrays)
    keys = sum(a.shape[0] for a in arrays)
    return pl.pallas_call(
        functools.partial(attend_kernel, names, first, last, n),
        out_shape=out_shape,
        in_specs=[smem, smem] + [vmem] * len(ins),
        out_specs=out_specs,
        cost_estimate=pl.CostEstimate(
            flops=4 * rows * keys * FW, bytes_accessed=keys * FW * 4 + rows * FW * 8, transcendentals=rows * keys * HG
        ),
        name="attend_" + "_".join(names),
    )(where, masks, *ins)


def on_device(queries, keys, values, positions, tile_masks, sink_index):
    rows = queries.shape[0]
    shards = lax.axis_size("tm")
    planes = shards // PLANE
    me = lax.axis_index("tm")
    x, y = me & 1, (me >> 1) & 1

    def swap(a, bit):
        return lax.ppermute(a, "tm", [(i, i ^ bit) for i in range(shards)])

    def climb(a, up):
        pairs = [(i, i + PLANE if up(i) else i - PLANE) for i in range(shards)]
        return lax.ppermute(a, "tm", [(i, t) for i, t in pairs if 0 <= t < shards])

    order = sink_index.reshape(2, 2, -1)
    order = jnp.where(y == 1, order, order[::-1])
    order = jnp.where(x == 1, order, order[:, ::-1]).reshape(-1)
    base = (me * rows).astype(jnp.int32).reshape(1)
    q_rot, own, give_y, give_x, mine = prepare(base, queries, keys, values, positions, order)

    where = jnp.stack([me, jnp.int32(shards)]).astype(jnp.int32)
    run = functools.partial(attend, where, tile_masks, q_rot)

    f = climb(own, lambda i: (i >> 1) & 1 == 1)
    got = swap(give_y, 2)
    by_y = swap(own, 2)
    by_x = swap(own, 1)
    g = climb(own, lambda i: (i >> 1) & 1 == 0)
    quarter = give_x.shape[0]
    got2 = swap(give_x + got[:quarter], 1)
    mine = mine + got[quarter:] + got2
    v = swap(f, 2)
    total = mine
    for k in range(1, planes):
        total = total + lax.ppermute(mine, "tm", [(i, (i + PLANE * k) % shards) for i in range(shards)])
    diag = swap(by_y, 1)
    w = climb(by_x, lambda i: i & 1 == 0)
    sink_x = swap(total, 1)
    r = swap(v, 1)
    half = jnp.concatenate([total, sink_x], axis=0)
    sink_y = swap(half, 2)
    sinks = jnp.concatenate([half, sink_y], axis=0)

    state = run([("own", own), ("F", f), ("X", by_x), ("Y", by_y), ("G", g)], None, False)
    state = run([("V", v), ("D", diag), ("W", w)], state, False)
    return run([("R", r), ("sink", sinks)], state, True)


def solution(mesh):
    in_specs = (
        P("tm", "heads"),
        P("tm", "heads"),
        P("tm", "heads"),
        P(None, "tm"),
        P("tm", None, None),
        P(),
    )
    return jax.shard_map(
        on_device, mesh=mesh, in_specs=in_specs, out_specs=P("tm", "heads"), check_vma=False
    )
```
